32 devices in a mesh: sx: 4 (over y, x), sy: 2 (over core), op: 4 (over z).
Axes of the slice: x: 2, y: 2, z: 4, core: 2. Of those that a mesh axis runs over, the one named last changes fastest.
Arguments:
- op_real: float32 [4, 2, 6144, 6144], P('sx', 'sy', 'op'), may hold values from -0.0546875 to 0.0546875
- op_imag: float32 [4, 2, 6144, 6144], P('sx', 'sy', 'op'), may hold values from -0.0546875 to 0.0546875
- coef_right: float32 [4, 2, 2, 6144], P('sx', 'sy', None, 'op'), may hold values from -3 to 3
- coef_upper: float32 [4, 2, 2, 6144], P('sx', 'sy', None, 'op'), may hold values from -3 to 3
- sources: float32 [4, 2, 2, 16, 6144], P('sx', 'sy', None, None, 'op'), may hold values from -6 to 6
Outputs:
- traces: float32 [4, 2, 2, 16, 6144], P('sx', 'sy', None, None, 'op')
The draws below stay inside these ranges and needn't reach their ends.
All inputs are finite; a program needn't handle non-finite values.
Results may differ from the reference program's by a relative error of at most 0.0003.
Values sent between devices are 32-bit elements; how exact they have to be, the bound alone decides.
A program may use at most 128 MiB of HBM per device.

```python
import jax
import jax.numpy as jnp
from jax import lax

M = 6144
SRC = 16
NCOL = 4
NROW = 2


def block_levels(own_key, extent, pieces, low, top_value):
    level = 1.0
    for axis_at, blocks in pieces:
        steps = jax.random.uniform(jax.random.fold_in(jax.random.fold_in(own_key, 6), axis_at), (blocks,), jnp.float32, low / len(pieces), top_value / len(pieces))
        level = level * jnp.repeat(jnp.exp(steps), extent[axis_at] // blocks).reshape((-1,) + (1,) * (len(extent) - 1 - axis_at))
    return level


def bell_draw(rng, dims, scale, reach, cuts=(), held_as=jnp.bfloat16):
    values = jax.random.normal(rng, dims, jnp.float32) * scale
    if len(cuts) > 0:
        values = block_levels(rng, dims, cuts, -0.22, 0.18) * values
    return jnp.clip(values, min=-reach, max=reach).astype(held_as)


def setup_inputs(seed: int = 0) -> dict:
    key_list = jax.random.split(jax.random.key(seed), 6)
    return {
        "op_real": bell_draw(key_list[0], (NCOL, NROW, M, M), (2 * M) ** -0.5, 0.0546875, ((0, 4), (1, 2), (2, 4)), jnp.float32),
        "op_imag": bell_draw(key_list[1], (NCOL, NROW, M, M), (2 * M) ** -0.5, 0.0546875, ((0, 4), (1, 2), (2, 4)), jnp.float32),
        "coef_right": bell_draw(key_list[2], (NCOL, NROW, 2, M), 0.5, 3.0, ((0, 4), (1, 2), (3, 4)), jnp.float32),
        "coef_upper": bell_draw(key_list[3], (NCOL, NROW, 2, M), 0.5, 3.0, ((0, 4), (1, 2), (3, 4)), jnp.float32),
        "sources": bell_draw(key_list[4], (NCOL, NROW, 2, SRC, M), 1.0, 6.0, ((0, 4), (1, 2), (4, 4)), jnp.float32),
    }


def contract(left, right):
    return lax.dot_general(left, right, (((1,), (1,)), ((), ())), precision=lax.Precision.HIGHEST, preferred_element_type=jnp.float32)


def complex_scale(coef, field):
    real_part = coef[0][None, :] * field[0] - coef[1][None, :] * field[1]
    imag_part = coef[0][None, :] * field[1] + coef[1][None, :] * field[0]
    return jnp.stack([real_part, imag_part])


def apply_operator(real_mat, imag_mat, field):
    real_part = contract(field[0], real_mat) - contract(field[1], imag_mat)
    imag_part = contract(field[0], imag_mat) + contract(field[1], real_mat)
    return jnp.stack([real_part, imag_part])


def reference(op_real, op_imag, coef_right, coef_upper, sources):
    result = [[None] * NROW for column_at in range(NCOL)]
    for column_at in range(NCOL):
        for row_at in range(NROW):
            incoming = sources[column_at, row_at]
            if column_at > 0:
                incoming = incoming + complex_scale(coef_right[column_at, row_at], result[column_at - 1][row_at])
            if row_at > 0:
                incoming = incoming + complex_scale(coef_upper[column_at, row_at], result[column_at][row_at - 1])
            result[column_at][row_at] = apply_operator(op_real[column_at, row_at], op_imag[column_at, row_at], incoming)
    return jnp.stack([jnp.stack(column_list) for column_list in result])
```

```python
import functools

import jax
import jax.numpy as jnp
from jax import lax
from jax.experimental import pallas as pl
from jax.experimental.pallas import tpu as pltpu
from jax.sharding import PartitionSpec as P

MESH = pl.DeviceIdType.MESH
LOAD_ROWS = 32
SLOTS = 3
LOW_SCALE = 2.0**20
F8 = jnp.float8_e4m3fn
F32 = jnp.float32
BF16 = jnp.bfloat16
NT = (((1,), (1,)), ((), ()))


def kernel(
    ncol, nrow, nop, groups, block,
    real_hbm, imag_hbm, right_ref, upper_ref, src_ref, out_ref,
    high, low, stage, gathered, xw, x8, inv, left_buf, below_buf, trace,
    load_sem, gsend, grecv, lsend, lrecv, usend, urecv,
):
    c = lax.axis_index("sx")
    r = lax.axis_index("sy")
    z = lax.axis_index("op")
    first = c + r == 0
    rows, width = real_hbm.shape
    srcs = src_ref.shape[1]
    group_rows = rows // groups
    chunks = rows // LOAD_ROWS
    per_block = block // LOAD_ROWS
    blocks = group_rows // block
    ops = (real_hbm, imag_hbm)

    def load(chunk, slot, k):
        at = pl.multiple_of(chunk * LOAD_ROWS, LOAD_ROWS)
        return pltpu.make_async_copy(
            ops[k].at[pl.ds(at, LOAD_ROWS), :], stage.at[slot, k], load_sem.at[slot, k]
        )

    for s in range(SLOTS):
        for k in range(2):
            load(s, s, k).start()

    barrier = pltpu.get_barrier_semaphore()
    for j in range(1, nop):
        pl.semaphore_signal(
            barrier, inc=1, device_id=(c, r, lax.rem(z + j, nop)), device_id_type=MESH
        )

    def greet(cond, cc, rr):
        @pl.when(cond)
        def _():
            pl.semaphore_signal(barrier, inc=1, device_id=(cc, rr, z), device_id_type=MESH)

    has_left, has_right = c > 0, c < ncol - 1
    has_below, has_above = r > 0, r < nrow - 1
    greet(has_left, c - 1, r)
    greet(has_right, c + 1, r)
    greet(has_below, c, r - 1)
    greet(has_above, c, r + 1)
    near = sum(jnp.where(cond, 1, 0) for cond in (has_left, has_right, has_below, has_above))
    pl.semaphore_wait(barrier, nop - 1 + near)

    def send_right(g):
        return pltpu.make_async_remote_copy(
            trace.at[g], left_buf.at[g], lsend.at[g], lrecv.at[g],
            device_id=(c + 1, r, z), device_id_type=MESH,
        )

    def send_up(g):
        return pltpu.make_async_remote_copy(
            trace.at[g], below_buf.at[g], usend.at[g], urecv.at[g],
            device_id=(c, r + 1, z), device_id_type=MESH,
        )

    def share(g, j):
        peer = lax.rem(z + j, nop)
        return pltpu.make_async_remote_copy(
            gathered.at[z, g], gathered.at[z, g], gsend.at[g, j], grecv.at[g, j],
            device_id=(c, r, peer), device_id_type=MESH,
        )

    def gather():
        for g in range(groups):
            cols = pl.ds(g * group_rows, group_rows)
            gathered[z, g] = src_ref[:, :, cols]

            def add(coef_ref, buf):
                cr = coef_ref[0:1, cols]
                ci = coef_ref[1:2, cols]
                gathered[z, g, 0] += cr * buf[g, 0] - ci * buf[g, 1]
                gathered[z, g, 1] += cr * buf[g, 1] + ci * buf[g, 0]

            @pl.when(has_left)
            def _():
                send_right(g).wait_recv()
                add(right_ref, left_buf)

            @pl.when(has_below)
            def _():
                send_up(g).wait_recv()
                add(upper_ref, below_buf)

            for j in range(1, nop):
                share(g, j).start()
        for g in range(groups):
            for j in range(1, nop):
                share(g, j).wait()

        def largest(step, top):
            zz, g = step // groups, lax.rem(step, groups)
            both = jnp.maximum(jnp.abs(gathered[zz, g, 0]), jnp.abs(gathered[zz, g, 1]))
            return jnp.maximum(top, jnp.max(both, axis=1, keepdims=True))

        top = lax.fori_loop(0, nop * groups, largest, jnp.zeros((srcs, 1), F32))
        top = jnp.maximum(top, 1e-30)
        inv[...] = jnp.broadcast_to(top * (1.0 / (256.0 * LOW_SCALE)), inv.shape)
        scale = 256.0 / top

        @pl.loop(0, nop * groups)
        def _(step):
            zz, g = step // groups, lax.rem(step, groups)
            at = pl.multiple_of(step * group_rows, group_rows)
            for k in range(2):
                value = gathered[zz, g, k]
                top_part = value.astype(BF16)
                xw[k * srcs:(k + 1) * srcs, pl.ds(at, group_rows)] = top_part
                xw[(2 + k) * srcs:(3 + k) * srcs, pl.ds(at, group_rows)] = (
                    value - top_part.astype(F32)
                ).astype(BF16)
            both = jnp.concatenate([gathered[zz, g, 0] * scale, gathered[zz, g, 1] * scale], axis=0)
            x8[:, pl.ds(at, group_rows)] = both.astype(F8)

    def convert(b):
        @pl.loop(0, per_block)
        def _(i):
            chunk = b * per_block + i
            slot = lax.rem(chunk, SLOTS)
            at = pl.multiple_of(chunk * LOAD_ROWS, LOAD_ROWS)
            for k in range(2):
                load(chunk, slot, k).wait()

                @pl.loop(0, width // 512)
                def _(q):
                    cols = pl.ds(pl.multiple_of(q * 512, 512), 512)
                    value = stage[slot, k, :, cols]
                    top_part = value.astype(BF16)
                    high[k, pl.ds(at, LOAD_ROWS), cols] = top_part
                    low[k, pl.ds(at, LOAD_ROWS), cols] = (
                        (value - top_part.astype(F32)) * LOW_SCALE
                    ).astype(F8)

            @pl.when(chunk + SLOTS < chunks)
            def _():
                for k in range(2):
                    load(chunk + SLOTS, slot, k).start()

    def multiply(g, b):
        at = pl.ds(pl.multiple_of((g * blocks + b) * block, block), block)
        here = pl.ds(pl.multiple_of(b * block, block), block)
        parts = []
        for k in range(2):
            big = lax.dot_general(xw[...], high[k, at, :], NT, preferred_element_type=F32)
            small = lax.dot_general(x8[...], low[k, at, :], NT, preferred_element_type=F32)
            factor = jnp.concatenate([inv[:, :1], inv[:, :1]], axis=0)
            parts.append(big[:2 * srcs] + (big[2 * srcs:] + small * factor))
        trace[g, 0, :, here] = parts[0][:srcs] - parts[1][srcs:]
        trace[g, 1, :, here] = parts[1][:srcs] + parts[0][srcs:]

    def publish(g):
        @pl.when(has_right)
        def _():
            send_right(g).start()

        @pl.when(has_above)
        def _():
            send_up(g).start()

        out_ref[:, :, g * group_rows:(g + 1) * group_rows] = trace[g]

    @pl.when(first)
    def _():
        gather()

    for phase in range(2):
        @pl.when(True if phase == 0 else jnp.logical_not(first))
        def _():
            if phase == 1:
                gather()
            for g in range(groups):
                @pl.loop(0, blocks)
                def _(b):
                    if phase == 0:
                        convert(g * blocks + b)

                        @pl.when(first)
                        def _():
                            multiply(g, b)
                    else:
                        multiply(g, b)
                if phase == 0:
                    @pl.when(first)
                    def _():
                        publish(g)
                else:
                    publish(g)

    for g in range(groups):
        @pl.when(has_right)
        def _():
            send_right(g).wait_send()

        @pl.when(has_above)
        def _():
            send_up(g).wait_send()


def solution(mesh):
    ncol, nrow, nop = (mesh.shape[a] for a in ("sx", "sy", "op"))

    def shards(op_real, op_imag, coef_right, coef_upper, sources):
        rows, width = op_real.shape[2:]
        srcs = sources.shape[3]
        groups = 3 if rows % 384 == 0 else 1
        group_rows = rows // groups
        block = 256 if group_rows % 256 == 0 else 128
        vmem = pl.BlockSpec(memory_space=pltpu.VMEM)
        hbm = pl.BlockSpec(memory_space=pl.ANY)
        dma = pltpu.SemaphoreType.DMA
        out = pl.pallas_call(
            functools.partial(kernel, ncol, nrow, nop, groups, block),
            out_shape=jax.ShapeDtypeStruct((2, srcs, rows), F32),
            in_specs=[hbm, hbm, vmem, vmem, vmem],
            out_specs=vmem,
            scratch_shapes=[
                pltpu.VMEM((2, rows, width), BF16),
                pltpu.VMEM((2, rows, width), F8),
                pltpu.VMEM((SLOTS, 2, LOAD_ROWS, width), F32),
                pltpu.VMEM((nop, groups, 2, srcs, group_rows), F32),
                pltpu.VMEM((4 * srcs, width), BF16),
                pltpu.VMEM((2 * srcs, width), F8),
                pltpu.VMEM((srcs, 128), F32),
                pltpu.VMEM((groups, 2, srcs, group_rows), F32),
                pltpu.VMEM((groups, 2, srcs, group_rows), F32),
                pltpu.VMEM((groups, 2, srcs, group_rows), F32),
                dma((SLOTS, 2)),
                dma((groups, nop)),
                dma((groups, nop)),
                dma((groups,)),
                dma((groups,)),
                dma((groups,)),
                dma((groups,)),
            ],
            compiler_params=pltpu.CompilerParams(
                collective_id=0, has_side_effects=True, vmem_limit_bytes=67043328
            ),
        )(op_real[0, 0], op_imag[0, 0], coef_right[0, 0], coef_upper[0, 0], sources[0, 0])
        return out[None, None]

    return jax.shard_map(
        shards,
        mesh=mesh,
        in_specs=(
            P("sx", "sy", "op", None),
            P("sx", "sy", "op", None),
            P("sx", "sy", None, "op"),
            P("sx", "sy", None, "op"),
            P("sx", "sy", None, None, "op"),
        ),
        out_specs=P("sx", "sy", None, None, "op"),
        check_vma=False,
    )
```
